32 devices in a mesh: gx: 8 (over y, x, core), gy: 4 (over z).
Axes of the slice: x: 2, y: 2, z: 4, core: 2. Of those that a mesh axis runs over, the one named last changes fastest.
Arguments:
- adjoint_source: float32 [4, 64, 256, 512], P(None, 'gx', 'gy'), may hold values from -40 to 40, as said below
- conductivity: float32 [64, 256, 512], P('gx', 'gy'), may hold values from 0.1 to 10
- electrodes: int32 [4], replicated, may hold values from 0 to 16383
Outputs:
- solution_field: float32 [4, 64, 256, 512], P(None, 'gx', 'gy')
- residual: float32 [4, 64, 256, 512], P(None, 'gx', 'gy')
The draws below stay inside these ranges and needn't reach their ends.
Inputs may be any that keep to these rules, and one draw needn't show every extreme that they name: `electrodes`: each entry is a surface cell index, its first coordinate times 256 plus its second. `adjoint_source`: drawn afresh cell by cell.
All inputs are finite; a program needn't handle non-finite values.
Results may differ from the reference program's by a relative error of at most 0.0003.
Values sent between devices are 32-bit elements; how exact they have to be, the bound alone decides.
A program may use at most 128 MiB of HBM per device.

```python
import math
import jax
import jax.numpy as jnp
from jax import lax

CZ = 512
SOURCES = 4
ITERS = 2
NX = 64
NY = 256


def draw_adjoint_source(key, part):
    key_base, key_column, key_cell = jax.random.split(key, 3)
    shape = (SOURCES, NX, NY, CZ)
    column_draw = jax.random.uniform(key_column, (SOURCES,), jnp.float32, 0.0, 1.0)
    column_level = (jnp.arange(SOURCES, dtype=jnp.float32) + column_draw) / SOURCES
    column = jnp.exp(column_level * math.log(10.0)).reshape(SOURCES, 1, 1, 1)
    cell = jnp.exp(jax.random.uniform(key_cell, (1, NX, NY, CZ), jnp.float32, 0.0, math.log(10.0)))
    position = jnp.arange(NX, dtype=jnp.float32) / max(NX - 1, 1)
    base = jax.random.truncated_normal(key_base, -6.0, 6.0, shape, jnp.float32)
    rise = jnp.exp(position * math.log(3.0))
    values = 0.1 * base * column * cell * rise[None, :, None, None]
    return jnp.clip(values, -40.0, 40.0)


def with_ends(values, rng, least, largest):
    dims = values.shape
    spot = [jax.random.randint(jax.random.fold_in(rng, axis), (), 0, dims[axis]) for axis in range(len(dims))]
    values = values.at[tuple(spot)].set(least)
    longest = dims.index(max(dims))
    spot[longest] = (spot[longest] + 1) % dims[longest]
    return values.at[tuple(spot)].set(largest)


def shard_levels(stream_key, dims, shards, least, high):
    gain = 1.0
    for dim, shards_of in shards:
        steps = jax.random.uniform(jax.random.fold_in(jax.random.fold_in(stream_key, 6), dim), (shards_of,), jnp.float32, least / len(shards), high / len(shards))
        gain = gain * jnp.repeat(jnp.exp(steps), dims[dim] // shards_of).reshape((-1,) + (1,) * (len(dims) - 1 - dim))
    return gain


def setup_inputs(seed: int = 0) -> dict:
    arg_keys = jax.random.split(jax.random.key(seed), 4)
    adjoint_source = draw_adjoint_source(jax.random.fold_in(arg_keys[3], 71), 0)
    conductivity = jnp.clip(jnp.exp(math.log(10.0) - 4.6051702 * jax.random.uniform(arg_keys[1], (NX, NY, CZ), jnp.float32) ** shard_levels(arg_keys[1], (NX, NY, CZ), ((0, 8), (1, 4)), -0.2, 0.2)), 0.1, 10.0)
    electrodes = with_ends(jax.random.randint(arg_keys[2], (SOURCES,), 0, NX * NY), jax.random.fold_in(arg_keys[2], 1), 0, (NX * NY) - 1).astype(jnp.int32)
    return dict(adjoint_source=adjoint_source, conductivity=conductivity, electrodes=electrodes)


def face_coefficients(padded):
    center = padded[1:-1, 1:-1, 1:-1]

    def face(neighbour):
        return jnp.where(neighbour > 0.0, 0.5 * (center + neighbour), center)
    return (face(padded[2:, 1:-1, 1:-1]), face(padded[:-2, 1:-1, 1:-1]), face(padded[1:-1, 2:, 1:-1]), face(padded[1:-1, :-2, 1:-1]), face(padded[1:-1, 1:-1, 2:]), face(padded[1:-1, 1:-1, :-2]))

def apply_operator(padded, coeffs):
    center = padded[:, 1:-1, 1:-1, 1:-1]
    others = (padded[:, 2:, 1:-1, 1:-1], padded[:, :-2, 1:-1, 1:-1], padded[:, 1:-1, 2:, 1:-1], padded[:, 1:-1, :-2, 1:-1], padded[:, 1:-1, 1:-1, 2:], padded[:, 1:-1, 1:-1, :-2])
    total = jnp.zeros(center.shape, jnp.float32)
    for coeff, other in zip(coeffs, others):
        total = total + coeff[None] * (center - other)
    return total

def gram(left, right):
    return jnp.einsum('ixyz,jxyz->ij', left, right, precision=lax.Precision.HIGHEST)

def combine(matrix, block):
    return jnp.einsum('ij,ixyz->jxyz', matrix, block, precision=lax.Precision.HIGHEST)

def small_solve(spd, rhs):
    factor = jnp.linalg.cholesky(spd)
    return jax.scipy.linalg.cho_solve((factor, True), rhs)

def reference(adjoint_source, conductivity, electrodes):
    coeffs = face_coefficients(jnp.pad(conductivity, 1))
    current = math.sqrt(NX * NY * CZ)
    row_x = (electrodes // NY).astype(jnp.int32)
    row_y = (electrodes % NY).astype(jnp.int32)
    mark_x = (jnp.arange(NX, dtype=jnp.int32)[None, :] == row_x[:, None]).astype(jnp.float32)
    mark_y = (jnp.arange(NY, dtype=jnp.int32)[None, :] == row_y[:, None]).astype(jnp.float32)
    spike = current * (mark_x[:, :, None] * mark_y[:, None, :])
    right_side = adjoint_source.at[:, :, :, 0].add(spike)
    solution_field = jnp.zeros_like(right_side)
    residual = right_side
    direction = right_side
    norm_now = gram(residual, residual)
    for step in range(ITERS):
        padded = jnp.pad(direction, ((0, 0), (1, 1), (1, 1), (1, 1)))
        image = apply_operator(padded, coeffs)
        curvature = gram(direction, image)
        alpha = small_solve(curvature, norm_now)
        solution_field = solution_field + combine(alpha, direction)
        residual = residual - combine(alpha, image)
        if step + 1 < ITERS:
            norm_next = gram(residual, residual)
            beta = small_solve(norm_now, norm_next)
            direction = residual + combine(beta, direction)
            norm_now = norm_next
    return (solution_field, residual)
```

```python
import functools
import math

import jax
import jax.numpy as jnp
from jax import lax
from jax.experimental import pallas as pl
from jax.experimental.pallas import tpu as pltpu
from jax.sharding import PartitionSpec as P

MESH = pl.DeviceIdType.MESH
F = 4
PAIRS = [(i, j) for i in range(F) for j in range(i, F)]
NP = len(PAIRS)
TILE = 8
LANES = 128


def remote(src, dst, send, recv, axis, index):
    return pltpu.make_async_remote_copy(
        src_ref=src, dst_ref=dst, send_sem=send, recv_sem=recv,
        device_id={axis: index}, device_id_type=MESH,
    )


def operator_kernel(
    nx, ny, current, adj, sig, elec, r_out, q_out, w_out, sums,
    R, Q, W, S, wt, edge, got, acc, part_x, part_y,
    local, xs, xr, ys, yr, ax_s, ax_r, ay_s, ay_r,
):
    cx, cy, cz = sig.shape
    total_y = ny * cy
    mx, my = lax.axis_index("gx"), lax.axis_index("gy")
    barrier = pltpu.get_barrier_semaphore()
    rows = pl.ds(TILE, cy)

    load_r = pltpu.make_async_copy(adj, R.at[:, pl.ds(1, cx), rows, :], local.at[0])
    load_s = pltpu.make_async_copy(sig, S.at[pl.ds(1, cx), rows, :], local.at[1])
    load_r.start()
    load_s.start()
    for axis, me, n in (("gx", mx, nx), ("gy", my, ny)):
        for d in range(1, n):
            pl.semaphore_signal(
                barrier, inc=1, device_id={axis: lax.rem(me + d, n)}, device_id_type=MESH
            )
    pl.semaphore_wait(barrier, nx + ny - 2)

    has_lo, has_hi = mx > 0, mx < nx - 1
    below, above = jnp.maximum(mx - 1, 0), jnp.minimum(mx + 1, nx - 1)
    y_lo, y_hi = my > 0, my < ny - 1
    left, right = jnp.maximum(my - 1, 0), jnp.minimum(my + 1, ny - 1)

    up_s = remote(sig.at[cx - 1], S.at[0, rows, :], xs.at[0], xr.at[0], "gx", above)
    dn_s = remote(sig.at[0], S.at[cx + 1, rows, :], xs.at[1], xr.at[1], "gx", below)
    up_r = remote(adj.at[:, cx - 1], R.at[:, 0, rows, :], xs.at[2], xr.at[2], "gx", above)
    dn_r = remote(adj.at[:, 0], R.at[:, cx + 1, rows, :], xs.at[3], xr.at[3], "gx", below)
    up_q = remote(Q.at[:, cx, rows, :], Q.at[:, 0, rows, :], xs.at[4], xr.at[4], "gx", above)
    dn_q = remote(Q.at[:, 1, rows, :], Q.at[:, cx + 1, rows, :], xs.at[5], xr.at[5], "gx", below)
    y_up = remote(edge.at[0], got.at[0], ys.at[0], yr.at[0], "gy", right)
    y_dn = remote(edge.at[1], got.at[1], ys.at[1], yr.at[1], "gy", left)
    y_up_q = remote(edge.at[2, pl.ds(0, F)], got.at[2, pl.ds(0, F)], ys.at[2], yr.at[2], "gy", right)
    y_dn_q = remote(edge.at[3, pl.ds(0, F)], got.at[3, pl.ds(0, F)], ys.at[3], yr.at[3], "gy", left)

    @pl.when(has_hi)
    def _():
        up_s.start()
        up_r.start()

    @pl.when(has_lo)
    def _():
        dn_s.start()
        dn_r.start()

    acc[...] = jnp.zeros_like(acc)
    edge_plane = jnp.zeros((cy, cz), jnp.float32)

    @pl.when(jnp.logical_not(has_lo))
    def _():
        S[0, rows, :] = edge_plane
        for f in range(F):
            R[f, 0, rows, :] = edge_plane
            Q[f, 0, rows, :] = edge_plane

    @pl.when(jnp.logical_not(has_hi))
    def _():
        S[cx + 1, rows, :] = edge_plane
        for f in range(F):
            R[f, cx + 1, rows, :] = edge_plane
            Q[f, cx + 1, rows, :] = edge_plane

    @pl.when(jnp.logical_not(y_lo))
    def _():
        got[0] = jnp.zeros(got.shape[1:], jnp.float32)
        got[2] = jnp.zeros(got.shape[1:], jnp.float32)

    @pl.when(jnp.logical_not(y_hi))
    def _():
        got[1] = jnp.zeros(got.shape[1:], jnp.float32)
        got[3] = jnp.zeros(got.shape[1:], jnp.float32)

    row_id = lax.broadcasted_iota(jnp.int32, (cy, LANES), 0)
    first = lax.broadcasted_iota(jnp.int32, (cy, LANES), 1) == 0

    def spike(x):
        cell = row_id + ((mx * cx + x - 1) * total_y + my * cy)
        for f in range(F):
            here = jnp.where(first & (cell == elec[f]), current, 0.0)
            R[f, x, rows, pl.ds(0, LANES)] = R[f, x, rows, pl.ds(0, LANES)] + here

    def pack(src, fields, base):
        def one(x, c):
            for k, ref in enumerate(src(x)):
                edge[base, k, pl.ds(x, 1), :] = ref(TILE + cy - 1)
                edge[base + 1, k, pl.ds(x, 1), :] = ref(TILE)
            return c
        lax.fori_loop(0, cx, one, 0)

    def row_r(f, x):
        return lambda y: R[f, x + 1, pl.ds(y, 1), :]

    def row_q(f, x):
        return lambda y: Q[f, x + 1, pl.ds(y, 1), :]

    def row_s(x):
        return lambda y: S[x + 1, pl.ds(y, 1), :]

    load_r.wait()

    def spike_loop(x, c):
        spike(x)
        return c

    lax.fori_loop(1, cx + 1, spike_loop, 0)
    load_s.wait()
    pack(lambda x: [row_r(f, x) for f in range(F)] + [row_s(x)], F + 1, 0)

    @pl.when(y_hi)
    def _():
        y_up.start()

    @pl.when(y_lo)
    def _():
        y_dn.start()

    keep_r = pltpu.make_async_copy(R.at[:, pl.ds(1, cx), rows, :], r_out, local.at[2])
    keep_r.start()

    @pl.when(y_lo)
    def _():
        y_up.wait_recv()

    @pl.when(y_hi)
    def _():
        y_dn.wait_recv()

    def unpack_first(x, c):
        for slot, y in ((0, TILE - 1), (1, TILE + cy)):
            for f in range(F):
                R[f, x + 1, pl.ds(y, 1), :] = got[slot, f, pl.ds(x, 1), :]
            S[x + 1, pl.ds(y, 1), :] = got[slot, F, pl.ds(x, 1), :]
        return c

    lax.fori_loop(0, cx, unpack_first, 0)

    lane = lax.broadcasted_iota(jnp.int32, (TILE, cz), 1)

    def add_grams(base, lefts, rights):
        for k, (i, j) in enumerate(PAIRS):
            prod = lefts[i] * rights[j]
            total = prod[:, :LANES]
            for c in range(LANES, cz, LANES):
                total = total + prod[:, c:c + LANES]
            acc[base + k] = acc[base + k] + total

    def apply(src, f, x, y, weights):
        mid = src[f, x, pl.ds(y, TILE), :]
        diag, xm, xp, ym, yp, zm, zp = weights
        out = diag * mid
        out = out - xm * src[f, x - 1, pl.ds(y, TILE), :]
        out = out - xp * src[f, x + 1, pl.ds(y, TILE), :]
        out = out - ym * src[f, x, pl.ds(y - 1, TILE), :]
        out = out - yp * src[f, x, pl.ds(y + 1, TILE), :]
        out = out - zm * pltpu.roll(mid, 1, axis=1)
        out = out - zp * pltpu.roll(mid, cz - 1, axis=1)
        return mid, out

    def first_plane(x):
        for t in range(cy // TILE):
            y = TILE + t * TILE
            here = S[x, pl.ds(y, TILE), :]
            others = (
                S[x - 1, pl.ds(y, TILE), :],
                S[x + 1, pl.ds(y, TILE), :],
                S[x, pl.ds(y - 1, TILE), :],
                S[x, pl.ds(y + 1, TILE), :],
                jnp.where(lane == 0, 0.0, pltpu.roll(here, 1, axis=1)),
                jnp.where(lane == cz - 1, 0.0, pltpu.roll(here, cz - 1, axis=1)),
            )
            diag = jnp.zeros_like(here)
            weights = []
            for other in others:
                inside = other > 0.0
                mean = 0.5 * (here + other)
                diag = diag + jnp.where(inside, mean, here)
                weights.append(jnp.where(inside, mean, 0.0))
            weights = [diag] + weights
            for k in range(7):
                wt[k, x - 1, pl.ds(t * TILE, TILE), :] = weights[k]
            rs, qs = [], []
            for f in range(F):
                mid, out = apply(R, f, x, y, weights)
                Q[f, x, pl.ds(y, TILE), :] = out
                rs.append(mid)
                qs.append(out)
            add_grams(0, rs, rs)
            add_grams(NP, rs, qs)

    def second_plane(x):
        for t in range(cy // TILE):
            y = TILE + t * TILE
            weights = [wt[k, x - 1, pl.ds(t * TILE, TILE), :] for k in range(7)]
            qs, ws = [], []
            for f in range(F):
                mid, out = apply(Q, f, x, y, weights)
                W[f, x - 1, pl.ds(t * TILE, TILE), :] = out
                qs.append(mid)
                ws.append(out)
            add_grams(2 * NP, qs, qs)
            add_grams(3 * NP, qs, ws)

    def run(plane):
        def one(x, c):
            plane(x)
            return c
        return one

    lax.fori_loop(2, cx, run(first_plane), 0)

    @pl.when(has_lo)
    def _():
        up_s.wait_recv()
        up_r.wait_recv()

    @pl.when(has_hi)
    def _():
        dn_s.wait_recv()
        dn_r.wait_recv()

    def ends(plane):
        def one(k, c):
            plane(k)
            return c
        return one

    lax.fori_loop(0, 2, ends(lambda k: spike(k * (cx + 1))), 0)
    lax.fori_loop(0, 2, ends(lambda k: first_plane(1 + k * (cx - 1))), 0)

    @pl.when(has_hi)
    def _():
        up_q.start()

    @pl.when(has_lo)
    def _():
        dn_q.start()

    pack(lambda x: [row_q(f, x) for f in range(F)], F, 2)

    @pl.when(y_hi)
    def _():
        y_up_q.start()

    @pl.when(y_lo)
    def _():
        y_dn_q.start()

    keep_q = pltpu.make_async_copy(Q.at[:, pl.ds(1, cx), rows, :], q_out, local.at[3])
    keep_q.start()

    @pl.when(y_lo)
    def _():
        y_up_q.wait_recv()

    @pl.when(y_hi)
    def _():
        y_dn_q.wait_recv()

    def unpack_second(x, c):
        for slot, y in ((2, TILE - 1), (3, TILE + cy)):
            for f in range(F):
                Q[f, x + 1, pl.ds(y, 1), :] = got[slot, f, pl.ds(x, 1), :]
        return c

    lax.fori_loop(0, cx, unpack_second, 0)
    lax.fori_loop(2, cx, run(second_plane), 0)

    @pl.when(has_lo)
    def _():
        up_q.wait_recv()

    @pl.when(has_hi)
    def _():
        dn_q.wait_recv()

    lax.fori_loop(0, 2, ends(lambda k: second_plane(1 + k * (cx - 1))), 0)
    keep_w = pltpu.make_async_copy(W, w_out, local.at[4])
    keep_w.start()

    part_x[mx] = jnp.sum(acc[...], axis=1)

    def exchange(buf, axis, me, n, sends, recvs):
        copies = [
            remote(buf.at[me], buf.at[me], sends.at[d - 1], recvs.at[d - 1], axis, lax.rem(me + d, n))
            for d in range(1, n)
        ]
        for copy in copies:
            copy.start()
        for d in range(1, n):
            src = lax.rem(me + n - d, n)
            remote(
                buf.at[me], buf.at[src], sends.at[d - 1], recvs.at[d - 1], axis, src
            ).wait_recv()
        total = buf[0]
        for k in range(1, n):
            total = total + buf[k]
        return copies, total

    copies_x, total_x = exchange(part_x, "gx", mx, nx, ax_s, ax_r)
    part_y[my] = total_x
    copies_y, total = exchange(part_y, "gy", my, ny, ay_s, ay_r)
    sums[...] = jnp.broadcast_to(jnp.sum(total, axis=1, keepdims=True), sums.shape)

    for copy in copies_x + copies_y:
        copy.wait_send()

    @pl.when(has_hi)
    def _():
        up_s.wait_send()
        up_r.wait_send()
        up_q.wait_send()

    @pl.when(has_lo)
    def _():
        dn_s.wait_send()
        dn_r.wait_send()
        dn_q.wait_send()

    @pl.when(y_hi)
    def _():
        y_up.wait_send()
        y_up_q.wait_send()

    @pl.when(y_lo)
    def _():
        y_dn.wait_send()
        y_dn_q.wait_send()

    keep_r.wait()
    keep_q.wait()
    keep_w.wait()


def mat(a, b):
    return [
        [sum(a[i][k] * b[k][j] for k in range(1, F)) + a[i][0] * b[0][j] for j in range(F)]
        for i in range(F)
    ]


def add(a, b):
    return [[a[i][j] + b[i][j] for j in range(F)] for i in range(F)]


def sub(a, b):
    return [[a[i][j] - b[i][j] for j in range(F)] for i in range(F)]


def turn(a):
    return [[a[j][i] for j in range(F)] for i in range(F)]


def spd_solve(a, b):
    low = [[None] * F for _ in range(F)]
    inv = [None] * F
    rest = [list(row) for row in a]
    for k in range(F):
        inv[k] = 1.0 / rest[k][k]
        for i in range(k + 1, F):
            low[i][k] = rest[i][k] * inv[k]
        for i in range(k + 1, F):
            for j in range(k + 1, i + 1):
                rest[i][j] = rest[i][j] - low[i][k] * rest[j][k]
    out = [list(row) for row in b]
    for i in range(F):
        for k in range(i):
            out[i] = [u - low[i][k] * v for u, v in zip(out[i], out[k])]
    out = [[u * inv[i] for u in out[i]] for i in range(F)]
    for i in reversed(range(F)):
        for k in range(i + 1, F):
            out[i] = [u - low[k][i] * v for u, v in zip(out[i], out[k])]
    return out


def finish_kernel(sums, r_ref, q_ref, w_ref, x_ref, e_ref, coef):
    @pl.when(pl.program_id(0) == 0)
    def _():
        grams = []
        for g in range(4):
            m = [[None] * F for _ in range(F)]
            for k, (i, j) in enumerate(PAIRS):
                m[i][j] = m[j][i] = sums[pl.ds(g * NP + k, 1), :]
            grams.append(m)
        s0, s1, s2, s3 = grams
        a0 = spd_solve(s1, s0)
        s1a, s2a = mat(s1, a0), mat(s2, a0)
        a0t = turn(a0)
        rr = add(sub(sub(s0, s1a), turn(s1a)), mat(a0t, s2a))
        cross = add(sub(sub(s1, s2a), turn(s2a)), mat(a0t, mat(s3, a0)))
        beta = spd_solve(s0, rr)
        curve = sub(cross, mat(turn(beta), mat(s1, beta)))
        a1 = spd_solve(curve, rr)
        m1 = add(add(a0, a1), mat(beta, a1))
        m2 = mat(a0, a1)
        for i in range(F):
            for j in range(F):
                coef[pl.ds(i * F + j, 1), :] = m1[i][j]
                coef[pl.ds(F * F + i * F + j, 1), :] = m2[i][j]

    cy, cz = r_ref.shape[2:]
    c1 = [[jnp.broadcast_to(coef[pl.ds(i * F + j, 1), :], (TILE, LANES)) for j in range(F)] for i in range(F)]
    c2 = [[jnp.broadcast_to(coef[pl.ds(F * F + i * F + j, 1), :], (TILE, LANES)) for j in range(F)] for i in range(F)]

    def tile(t, c):
        y = pl.ds(pl.multiple_of(t * TILE, TILE), TILE)
        for z in range(0, cz, LANES):
            at = pl.ds(z, LANES)
            rs = [r_ref[f, 0, y, at] for f in range(F)]
            qs = [q_ref[f, 0, y, at] for f in range(F)]
            ws = [w_ref[f, 0, y, at] for f in range(F)]
            for j in range(F):
                field = rs[0] * c1[0][j] - qs[0] * c2[0][j]
                left = rs[j] - qs[0] * c1[0][j] + ws[0] * c2[0][j]
                for i in range(1, F):
                    field = field + rs[i] * c1[i][j] - qs[i] * c2[i][j]
                    left = left - qs[i] * c1[i][j] + ws[i] * c2[i][j]
                x_ref[j, 0, y, at] = field
                e_ref[j, 0, y, at] = left
        return c

    lax.fori_loop(0, cy // TILE, tile, 0)


def shards(nx, ny, adj, sig, elec):
    cx, cy, cz = sig.shape
    current = math.sqrt(nx * cx * ny * cy * cz)
    block = jax.ShapeDtypeStruct(adj.shape, jnp.float32)
    hbm = pl.BlockSpec(memory_space=pl.ANY)
    vmem = pl.BlockSpec(memory_space=pltpu.VMEM)
    padded = (cx + 2, cy + 2 * TILE, cz)
    dma = pltpu.SemaphoreType.DMA
    r, q, w, sums = pl.pallas_call(
        functools.partial(operator_kernel, nx, ny, current),
        out_shape=(block, block, block, jax.ShapeDtypeStruct((4 * NP, LANES), jnp.float32)),
        in_specs=[hbm, hbm, pl.BlockSpec(memory_space=pltpu.SMEM)],
        out_specs=(hbm, hbm, hbm, vmem),
        scratch_shapes=[
            pltpu.VMEM((F,) + padded, jnp.float32),
            pltpu.VMEM((F,) + padded, jnp.float32),
            pltpu.VMEM((F, cx, cy, cz), jnp.float32),
            pltpu.VMEM(padded, jnp.float32),
            pltpu.VMEM((7, cx, cy, cz), jnp.float32),
            pltpu.VMEM((4, F + 1, cx, cz), jnp.float32),
            pltpu.VMEM((4, F + 1, cx, cz), jnp.float32),
            pltpu.VMEM((4 * NP, TILE, LANES), jnp.float32),
            pltpu.VMEM((nx, 4 * NP, LANES), jnp.float32),
            pltpu.VMEM((ny, 4 * NP, LANES), jnp.float32),
            dma((5,)), dma((6,)), dma((6,)), dma((4,)), dma((4,)),
            dma((max(nx - 1, 1),)), dma((max(nx - 1, 1),)),
            dma((max(ny - 1, 1),)), dma((max(ny - 1, 1),)),
        ],
        compiler_params=pltpu.CompilerParams(collective_id=0, has_side_effects=True),
    )(adj, sig, elec)
    slab = pl.BlockSpec((F, 1, cy, cz), lambda x: (0, x, 0, 0))
    return pl.pallas_call(
        finish_kernel,
        grid=(cx,),
        out_shape=(block, block),
        in_specs=[pl.BlockSpec((4 * NP, LANES), lambda x: (0, 0)), slab, slab, slab],
        out_specs=(slab, slab),
        scratch_shapes=[pltpu.VMEM((2 * F * F, LANES), jnp.float32)],
    )(sums, r, q, w)


def solution(mesh):
    placed = (P(None, "gx", "gy", None), P("gx", "gy", None), P())
    return jax.shard_map(
        functools.partial(shards, mesh.shape["gx"], mesh.shape["gy"]),
        mesh=mesh,
        in_specs=placed,
        out_specs=(P(None, "gx", "gy", None), P(None, "gx", "gy", None)),
        check_vma=False,
    )
```

```python
import functools
import math

import jax
import jax.numpy as jnp
from jax import lax
from jax.experimental import pallas as pl
from jax.experimental.pallas import tpu as pltpu
from jax.sharding import PartitionSpec as P

MESH = pl.DeviceIdType.MESH
F = 4
PAIRS = [(i, j) for i in range(F) for j in range(i, F)]
NP = len(PAIRS)
TILE = 8
GRANT_A = 15 * 1024 * 1024
GRANT_B = 5 * 1024 * 1024
LANES = 128


def remote(src, dst, send, recv, axis, index):
    return pltpu.make_async_remote_copy(
        src_ref=src, dst_ref=dst, send_sem=send, recv_sem=recv,
        device_id={axis: index}, device_id_type=MESH,
    )


def operator_kernel(
    nx, ny, current, adj, sig, elec, R, Q, W, sums,
    S, wt, edge, got, acc, part_x, part_y,
    local, xs, xr, ys, yr, ax_s, ax_r, ay_s, ay_r,
):
    cx, cy, cz = sig.shape
    total_y = ny * cy
    mx, my = lax.axis_index("gx"), lax.axis_index("gy")
    barrier = pltpu.get_barrier_semaphore()
    rows = pl.ds(TILE, cy)

    load_r = pltpu.make_async_copy(adj, R.at[:, pl.ds(1, cx), rows, :], local.at[0])
    load_s = pltpu.make_async_copy(sig, S.at[pl.ds(1, cx), rows, :], local.at[1])
    load_r.start()
    load_s.start()
    for axis, me, n in (("gx", mx, nx), ("gy", my, ny)):
        for d in range(1, n):
            pl.semaphore_signal(
                barrier, inc=1, device_id={axis: lax.rem(me + d, n)}, device_id_type=MESH
            )
    pl.semaphore_wait(barrier, nx + ny - 2)

    has_lo, has_hi = mx > 0, mx < nx - 1
    below, above = jnp.maximum(mx - 1, 0), jnp.minimum(mx + 1, nx - 1)
    y_lo, y_hi = my > 0, my < ny - 1
    left, right = jnp.maximum(my - 1, 0), jnp.minimum(my + 1, ny - 1)

    up_s = remote(sig.at[cx - 1], S.at[0, rows, :], xs.at[0], xr.at[0], "gx", above)
    dn_s = remote(sig.at[0], S.at[cx + 1, rows, :], xs.at[1], xr.at[1], "gx", below)
    up_r = remote(adj.at[:, cx - 1], R.at[:, 0, rows, :], xs.at[2], xr.at[2], "gx", above)
    dn_r = remote(adj.at[:, 0], R.at[:, cx + 1, rows, :], xs.at[3], xr.at[3], "gx", below)
    up_q = remote(Q.at[:, cx, rows, :], Q.at[:, 0, rows, :], xs.at[4], xr.at[4], "gx", above)
    dn_q = remote(Q.at[:, 1, rows, :], Q.at[:, cx + 1, rows, :], xs.at[5], xr.at[5], "gx", below)
    y_up = remote(edge.at[0], got.at[0], ys.at[0], yr.at[0], "gy", right)
    y_dn = remote(edge.at[1], got.at[1], ys.at[1], yr.at[1], "gy", left)
    y_up_q = remote(edge.at[2, pl.ds(0, F)], got.at[2, pl.ds(0, F)], ys.at[2], yr.at[2], "gy", right)
    y_dn_q = remote(edge.at[3, pl.ds(0, F)], got.at[3, pl.ds(0, F)], ys.at[3], yr.at[3], "gy", left)

    @pl.when(has_hi)
    def _():
        up_s.start()
        up_r.start()

    @pl.when(has_lo)
    def _():
        dn_s.start()
        dn_r.start()

    acc[...] = jnp.zeros_like(acc)
    edge_plane = jnp.zeros((cy, cz), jnp.float32)

    @pl.when(jnp.logical_not(has_lo))
    def _():
        S[0, rows, :] = edge_plane
        for f in range(F):
            R[f, 0, rows, :] = edge_plane
            Q[f, 0, rows, :] = edge_plane

    @pl.when(jnp.logical_not(has_hi))
    def _():
        S[cx + 1, rows, :] = edge_plane
        for f in range(F):
            R[f, cx + 1, rows, :] = edge_plane
            Q[f, cx + 1, rows, :] = edge_plane

    @pl.when(jnp.logical_not(y_lo))
    def _():
        got[0] = jnp.zeros(got.shape[1:], jnp.float32)
        got[2] = jnp.zeros(got.shape[1:], jnp.float32)

    @pl.when(jnp.logical_not(y_hi))
    def _():
        got[1] = jnp.zeros(got.shape[1:], jnp.float32)
        got[3] = jnp.zeros(got.shape[1:], jnp.float32)

    row_id = lax.broadcasted_iota(jnp.int32, (cy, LANES), 0)
    first = lax.broadcasted_iota(jnp.int32, (cy, LANES), 1) == 0

    def spike(x):
        cell = row_id + ((mx * cx + x - 1) * total_y + my * cy)
        for f in range(F):
            here = jnp.where(first & (cell == elec[f]), current, 0.0)
            R[f, x, rows, pl.ds(0, LANES)] = R[f, x, rows, pl.ds(0, LANES)] + here

    def pack(src, fields, base):
        def one(x, c):
            for k, ref in enumerate(src(x)):
                edge[base, k, pl.ds(x, 1), :] = ref(TILE + cy - 1)
                edge[base + 1, k, pl.ds(x, 1), :] = ref(TILE)
            return c
        lax.fori_loop(0, cx, one, 0)

    def row_r(f, x):
        return lambda y: R[f, x + 1, pl.ds(y, 1), :]

    def row_q(f, x):
        return lambda y: Q[f, x + 1, pl.ds(y, 1), :]

    def row_s(x):
        return lambda y: S[x + 1, pl.ds(y, 1), :]

    load_r.wait()

    def spike_loop(x, c):
        spike(x)
        return c

    lax.fori_loop(1, cx + 1, spike_loop, 0)
    load_s.wait()
    pack(lambda x: [row_r(f, x) for f in range(F)] + [row_s(x)], F + 1, 0)

    @pl.when(y_hi)
    def _():
        y_up.start()

    @pl.when(y_lo)
    def _():
        y_dn.start()

    @pl.when(y_lo)
    def _():
        y_up.wait_recv()

    @pl.when(y_hi)
    def _():
        y_dn.wait_recv()

    def unpack_first(x, c):
        for slot, y in ((0, TILE - 1), (1, TILE + cy)):
            for f in range(F):
                R[f, x + 1, pl.ds(y, 1), :] = got[slot, f, pl.ds(x, 1), :]
            S[x + 1, pl.ds(y, 1), :] = got[slot, F, pl.ds(x, 1), :]
        return c

    lax.fori_loop(0, cx, unpack_first, 0)

    lane = lax.broadcasted_iota(jnp.int32, (TILE, cz), 1)

    def add_grams(base, lefts, rights):
        for k, (i, j) in enumerate(PAIRS):
            prod = lefts[i] * rights[j]
            total = prod[:, :LANES]
            for c in range(LANES, cz, LANES):
                total = total + prod[:, c:c + LANES]
            acc[base + k] = acc[base + k] + total

    def apply(src, f, x, y, weights):
        mid = src[f, x, pl.ds(y, TILE), :]
        diag, xm, xp, ym, yp, zm, zp = weights
        out = diag * mid
        out = out - xm * src[f, x - 1, pl.ds(y, TILE), :]
        out = out - xp * src[f, x + 1, pl.ds(y, TILE), :]
        out = out - ym * src[f, x, pl.ds(y - 1, TILE), :]
        out = out - yp * src[f, x, pl.ds(y + 1, TILE), :]
        out = out - zm * pltpu.roll(mid, 1, axis=1)
        out = out - zp * pltpu.roll(mid, cz - 1, axis=1)
        return mid, out

    def first_plane(x):
        for t in range(cy // TILE):
            y = TILE + t * TILE
            here = S[x, pl.ds(y, TILE), :]
            others = (
                S[x - 1, pl.ds(y, TILE), :],
                S[x + 1, pl.ds(y, TILE), :],
                S[x, pl.ds(y - 1, TILE), :],
                S[x, pl.ds(y + 1, TILE), :],
                jnp.where(lane == 0, 0.0, pltpu.roll(here, 1, axis=1)),
                jnp.where(lane == cz - 1, 0.0, pltpu.roll(here, cz - 1, axis=1)),
            )
            diag = jnp.zeros_like(here)
            weights = []
            for other in others:
                inside = other > 0.0
                mean = 0.5 * (here + other)
                diag = diag + jnp.where(inside, mean, here)
                weights.append(jnp.where(inside, mean, 0.0))
            weights = [diag] + weights
            for k in range(7):
                wt[k, x - 1, pl.ds(t * TILE, TILE), :] = weights[k]
            rs, qs = [], []
            for f in range(F):
                mid, out = apply(R, f, x, y, weights)
                Q[f, x, pl.ds(y, TILE), :] = out
                rs.append(mid)
                qs.append(out)
            add_grams(0, rs, rs)
            add_grams(NP, rs, qs)

    def second_plane(x):
        for t in range(cy // TILE):
            y = TILE + t * TILE
            weights = [wt[k, x - 1, pl.ds(t * TILE, TILE), :] for k in range(7)]
            qs, ws = [], []
            for f in range(F):
                mid, out = apply(Q, f, x, y, weights)
                W[f, x - 1, pl.ds(t * TILE, TILE), :] = out
                qs.append(mid)
                ws.append(out)
            add_grams(2 * NP, qs, qs)
            add_grams(3 * NP, qs, ws)

    def run(plane):
        def one(x, c):
            plane(x)
            return c
        return one

    lax.fori_loop(2, cx, run(first_plane), 0)

    @pl.when(has_lo)
    def _():
        up_s.wait_recv()
        up_r.wait_recv()

    @pl.when(has_hi)
    def _():
        dn_s.wait_recv()
        dn_r.wait_recv()

    def ends(plane):
        def one(k, c):
            plane(k)
            return c
        return one

    lax.fori_loop(0, 2, ends(lambda k: spike(k * (cx + 1))), 0)
    lax.fori_loop(0, 2, ends(lambda k: first_plane(1 + k * (cx - 1))), 0)

    @pl.when(has_hi)
    def _():
        up_q.start()

    @pl.when(has_lo)
    def _():
        dn_q.start()

    pack(lambda x: [row_q(f, x) for f in range(F)], F, 2)

    @pl.when(y_hi)
    def _():
        y_up_q.start()

    @pl.when(y_lo)
    def _():
        y_dn_q.start()

    @pl.when(y_lo)
    def _():
        y_up_q.wait_recv()

    @pl.when(y_hi)
    def _():
        y_dn_q.wait_recv()

    def unpack_second(x, c):
        for slot, y in ((2, TILE - 1), (3, TILE + cy)):
            for f in range(F):
                Q[f, x + 1, pl.ds(y, 1), :] = got[slot, f, pl.ds(x, 1), :]
        return c

    lax.fori_loop(0, cx, unpack_second, 0)
    lax.fori_loop(2, cx, run(second_plane), 0)

    @pl.when(has_lo)
    def _():
        up_q.wait_recv()

    @pl.when(has_hi)
    def _():
        dn_q.wait_recv()

    lax.fori_loop(0, 2, ends(lambda k: second_plane(1 + k * (cx - 1))), 0)

    part_x[mx] = jnp.sum(acc[...], axis=1)

    def exchange(buf, axis, me, n, sends, recvs):
        copies = [
            remote(buf.at[me], buf.at[me], sends.at[d - 1], recvs.at[d - 1], axis, lax.rem(me + d, n))
            for d in range(1, n)
        ]
        for copy in copies:
            copy.start()
        for d in range(1, n):
            src = lax.rem(me + n - d, n)
            remote(
                buf.at[me], buf.at[src], sends.at[d - 1], recvs.at[d - 1], axis, src
            ).wait_recv()
        total = buf[0]
        for k in range(1, n):
            total = total + buf[k]
        return copies, total

    copies_x, total_x = exchange(part_x, "gx", mx, nx, ax_s, ax_r)
    part_y[my] = total_x
    copies_y, total = exchange(part_y, "gy", my, ny, ay_s, ay_r)
    sums[...] = jnp.broadcast_to(jnp.sum(total, axis=1, keepdims=True), sums.shape)

    for copy in copies_x + copies_y:
        copy.wait_send()

    @pl.when(has_hi)
    def _():
        up_s.wait_send()
        up_r.wait_send()
        up_q.wait_send()

    @pl.when(has_lo)
    def _():
        dn_s.wait_send()
        dn_r.wait_send()
        dn_q.wait_send()

    @pl.when(y_hi)
    def _():
        y_up.wait_send()
        y_up_q.wait_send()

    @pl.when(y_lo)
    def _():
        y_dn.wait_send()
        y_dn_q.wait_send()


def mat(a, b):
    return [
        [sum(a[i][k] * b[k][j] for k in range(1, F)) + a[i][0] * b[0][j] for j in range(F)]
        for i in range(F)
    ]


def add(a, b):
    return [[a[i][j] + b[i][j] for j in range(F)] for i in range(F)]


def sub(a, b):
    return [[a[i][j] - b[i][j] for j in range(F)] for i in range(F)]


def turn(a):
    return [[a[j][i] for j in range(F)] for i in range(F)]


def spd_solve(a, b):
    low = [[None] * F for _ in range(F)]
    inv = [None] * F
    rest = [list(row) for row in a]
    for k in range(F):
        inv[k] = 1.0 / rest[k][k]
        for i in range(k + 1, F):
            low[i][k] = rest[i][k] * inv[k]
        for i in range(k + 1, F):
            for j in range(k + 1, i + 1):
                rest[i][j] = rest[i][j] - low[i][k] * rest[j][k]
    out = [list(row) for row in b]
    for i in range(F):
        for k in range(i):
            out[i] = [u - low[i][k] * v for u, v in zip(out[i], out[k])]
    out = [[u * inv[i] for u in out[i]] for i in range(F)]
    for i in reversed(range(F)):
        for k in range(i + 1, F):
            out[i] = [u - low[k][i] * v for u, v in zip(out[i], out[k])]
    return out


def finish_kernel(sums, r_ref, q_ref, w_ref, x_ref, e_ref, coef):
    @pl.when(pl.program_id(0) == 0)
    def _():
        grams = []
        for g in range(4):
            m = [[None] * F for _ in range(F)]
            for k, (i, j) in enumerate(PAIRS):
                m[i][j] = m[j][i] = sums[pl.ds(g * NP + k, 1), :]
            grams.append(m)
        s0, s1, s2, s3 = grams
        a0 = spd_solve(s1, s0)
        s1a, s2a = mat(s1, a0), mat(s2, a0)
        a0t = turn(a0)
        rr = add(sub(sub(s0, s1a), turn(s1a)), mat(a0t, s2a))
        cross = add(sub(sub(s1, s2a), turn(s2a)), mat(a0t, mat(s3, a0)))
        beta = spd_solve(s0, rr)
        curve = sub(cross, mat(turn(beta), mat(s1, beta)))
        a1 = spd_solve(curve, rr)
        m1 = add(add(a0, a1), mat(beta, a1))
        m2 = mat(a0, a1)
        for i in range(F):
            for j in range(F):
                coef[pl.ds(i * F + j, 1), :] = m1[i][j]
                coef[pl.ds(F * F + i * F + j, 1), :] = m2[i][j]

    x = pl.program_id(0)
    cy, cz = w_ref.shape[2:]
    c1 = [[jnp.broadcast_to(coef[pl.ds(i * F + j, 1), :], (TILE, LANES)) for j in range(F)] for i in range(F)]
    c2 = [[jnp.broadcast_to(coef[pl.ds(F * F + i * F + j, 1), :], (TILE, LANES)) for j in range(F)] for i in range(F)]

    def tile(t, c):
        y = pl.ds(pl.multiple_of(t * TILE, TILE), TILE)
        wide_y = pl.ds(pl.multiple_of(t * TILE + TILE, TILE), TILE)
        for z in range(0, cz, LANES):
            at = pl.ds(z, LANES)
            rs = [r_ref[f, x + 1, wide_y, at] for f in range(F)]
            qs = [q_ref[f, x + 1, wide_y, at] for f in range(F)]
            ws = [w_ref[f, x, y, at] for f in range(F)]
            for j in range(F):
                field = rs[0] * c1[0][j] - qs[0] * c2[0][j]
                left = rs[j] - qs[0] * c1[0][j] + ws[0] * c2[0][j]
                for i in range(1, F):
                    field = field + rs[i] * c1[i][j] - qs[i] * c2[i][j]
                    left = left - qs[i] * c1[i][j] + ws[i] * c2[i][j]
                x_ref[j, 0, y, at] = field
                e_ref[j, 0, y, at] = left
        return c

    lax.fori_loop(0, cy // TILE, tile, 0)


def shards(nx, ny, adj, sig, elec):
    cx, cy, cz = sig.shape
    current = math.sqrt(nx * cx * ny * cy * cz)
    block = jax.ShapeDtypeStruct(adj.shape, jnp.float32)
    hbm = pl.BlockSpec(memory_space=pltpu.HBM)
    vmem = pl.BlockSpec(memory_space=pltpu.VMEM)
    padded = (cx + 2, cy + 2 * TILE, cz)
    wide = jax.ShapeDtypeStruct((F,) + padded, jnp.float32)
    dma = pltpu.SemaphoreType.DMA
    adj = pltpu.with_memory_space_constraint(adj, pltpu.HBM)
    sig = pltpu.with_memory_space_constraint(sig, pltpu.HBM)
    r, q, w, sums = pl.pallas_call(
        functools.partial(operator_kernel, nx, ny, current),
        out_shape=(wide, wide, block, jax.ShapeDtypeStruct((4 * NP, LANES), jnp.float32)),
        in_specs=[hbm, hbm, pl.BlockSpec(memory_space=pltpu.SMEM)],
        out_specs=(vmem, vmem, vmem, vmem),
        scratch_shapes=[
            pltpu.VMEM(padded, jnp.float32),
            pltpu.VMEM((7, cx, cy, cz), jnp.float32),
            pltpu.VMEM((4, F + 1, cx, cz), jnp.float32),
            pltpu.VMEM((4, F + 1, cx, cz), jnp.float32),
            pltpu.VMEM((4 * NP, TILE, LANES), jnp.float32),
            pltpu.VMEM((nx, 4 * NP, LANES), jnp.float32),
            pltpu.VMEM((ny, 4 * NP, LANES), jnp.float32),
            dma((2,)), dma((6,)), dma((6,)), dma((4,)), dma((4,)),
            dma((max(nx - 1, 1),)), dma((max(nx - 1, 1),)),
            dma((max(ny - 1, 1),)), dma((max(ny - 1, 1),)),
        ],
        compiler_params=pltpu.CompilerParams(collective_id=0, has_side_effects=True, vmem_limit_bytes=GRANT_A),
    )(adj, sig, elec)
    slab = pl.BlockSpec((F, 1, cy, cz), lambda x: (0, x, 0, 0))
    return pl.pallas_call(
        finish_kernel,
        grid=(cx,),
        out_shape=(block, block),
        in_specs=[vmem, vmem, vmem, vmem],
        out_specs=(slab, slab),
        scratch_shapes=[pltpu.VMEM((2 * F * F, LANES), jnp.float32)],
        compiler_params=pltpu.CompilerParams(vmem_limit_bytes=GRANT_B),
    )(sums, r, q, w)


def solution(mesh):
    placed = (P(None, "gx", "gy", None), P("gx", "gy", None), P())
    return jax.shard_map(
        functools.partial(shards, mesh.shape["gx"], mesh.shape["gy"]),
        mesh=mesh,
        in_specs=placed,
        out_specs=(P(None, "gx", "gy", None), P(None, "gx", "gy", None)),
        check_vma=False,
    )
```

```python
import functools
import math

import jax
import jax.numpy as jnp
from jax import lax
from jax.experimental import pallas as pl
from jax.experimental.pallas import tpu as pltpu
from jax.sharding import PartitionSpec as P

MESH = pl.DeviceIdType.MESH
F = 4
PAIRS = [(i, j) for i in range(F) for j in range(i, F)]
NP = len(PAIRS)
TILE = 8
GRANT_A = 15 * 1024 * 1024
GRANT_B = 5 * 1024 * 1024
LANES = 128


def remote(src, dst, send, recv, axis, index):
    return pltpu.make_async_remote_copy(
        src_ref=src, dst_ref=dst, send_sem=send, recv_sem=recv,
        device_id={axis: index}, device_id_type=MESH,
    )


def operator_kernel(
    nx, ny, current, adj, sig, elec, R, Q, W, sums,
    S, wt, edge, got, acc, part_x, part_y,
    local, xs, xr, ys, yr, ax_s, ax_r, ay_s, ay_r,
):
    cx, cy, cz = sig.shape
    total_y = ny * cy
    mx, my = lax.axis_index("gx"), lax.axis_index("gy")
    barrier = pltpu.get_barrier_semaphore()
    rows = pl.ds(TILE, cy)

    load_r = pltpu.make_async_copy(adj, R.at[:, pl.ds(1, cx), rows, :], local.at[0])
    load_s = pltpu.make_async_copy(sig, S.at[pl.ds(1, cx), rows, :], local.at[1])
    load_r.start()
    load_s.start()
    for axis, me, n in (("gx", mx, nx), ("gy", my, ny)):
        for d in range(1, n):
            pl.semaphore_signal(
                barrier, inc=1, device_id={axis: lax.rem(me + d, n)}, device_id_type=MESH
            )
    pl.semaphore_wait(barrier, nx + ny - 2)

    has_lo, has_hi = mx > 0, mx < nx - 1
    below, above = jnp.maximum(mx - 1, 0), jnp.minimum(mx + 1, nx - 1)
    y_lo, y_hi = my > 0, my < ny - 1
    left, right = jnp.maximum(my - 1, 0), jnp.minimum(my + 1, ny - 1)

    up_s = remote(sig.at[cx - 1], S.at[0, rows, :], xs.at[0], xr.at[0], "gx", above)
    dn_s = remote(sig.at[0], S.at[cx + 1, rows, :], xs.at[1], xr.at[1], "gx", below)
    up_r, dn_r, up_q, dn_q = [], [], [], []
    for f in range(F):
        a = 2 + 4 * f
        up_r.append(remote(adj.at[f, cx - 1], R.at[f, 0, rows, :], xs.at[a], xr.at[a], "gx", above))
        dn_r.append(remote(adj.at[f, 0], R.at[f, cx + 1, rows, :], xs.at[a + 1], xr.at[a + 1], "gx", below))
        up_q.append(remote(Q.at[f, cx, rows, :], Q.at[f, 0, rows, :], xs.at[a + 2], xr.at[a + 2], "gx", above))
        dn_q.append(remote(Q.at[f, 1, rows, :], Q.at[f, cx + 1, rows, :], xs.at[a + 3], xr.at[a + 3], "gx", below))
    y_up = remote(edge.at[0], got.at[0], ys.at[0], yr.at[0], "gy", right)
    y_dn = remote(edge.at[1], got.at[1], ys.at[1], yr.at[1], "gy", left)
    y_up_q = remote(edge.at[2, pl.ds(0, F)], got.at[2, pl.ds(0, F)], ys.at[2], yr.at[2], "gy", right)
    y_dn_q = remote(edge.at[3, pl.ds(0, F)], got.at[3, pl.ds(0, F)], ys.at[3], yr.at[3], "gy", left)

    @pl.when(has_hi)
    def _():
        up_s.start()
        for copy in up_r:
            copy.start()

    @pl.when(has_lo)
    def _():
        dn_s.start()
        for copy in dn_r:
            copy.start()

    acc[...] = jnp.zeros_like(acc)
    edge_plane = jnp.zeros((cy, cz), jnp.float32)

    @pl.when(jnp.logical_not(has_lo))
    def _():
        S[0, rows, :] = edge_plane
        for f in range(F):
            R[f, 0, rows, :] = edge_plane
            Q[f, 0, rows, :] = edge_plane

    @pl.when(jnp.logical_not(has_hi))
    def _():
        S[cx + 1, rows, :] = edge_plane
        for f in range(F):
            R[f, cx + 1, rows, :] = edge_plane
            Q[f, cx + 1, rows, :] = edge_plane

    @pl.when(jnp.logical_not(y_lo))
    def _():
        got[0] = jnp.zeros(got.shape[1:], jnp.float32)
        got[2] = jnp.zeros(got.shape[1:], jnp.float32)

    @pl.when(jnp.logical_not(y_hi))
    def _():
        got[1] = jnp.zeros(got.shape[1:], jnp.float32)
        got[3] = jnp.zeros(got.shape[1:], jnp.float32)

    row_id = lax.broadcasted_iota(jnp.int32, (cy, LANES), 0)
    first = lax.broadcasted_iota(jnp.int32, (cy, LANES), 1) == 0

    def spike(x, fields=range(F)):
        cell = row_id + ((mx * cx + x - 1) * total_y + my * cy)
        for f in fields:
            here = jnp.where(first & (cell == elec[f]), current, 0.0)
            R[f, x, rows, pl.ds(0, LANES)] = R[f, x, rows, pl.ds(0, LANES)] + here

    def pack(src, fields, base):
        def one(x, c):
            for k, ref in enumerate(src(x)):
                edge[base, k, pl.ds(x, 1), :] = ref(TILE + cy - 1)
                edge[base + 1, k, pl.ds(x, 1), :] = ref(TILE)
            return c
        lax.fori_loop(0, cx, one, 0)

    def row_r(f, x):
        return lambda y: R[f, x + 1, pl.ds(y, 1), :]

    def row_q(f, x):
        return lambda y: Q[f, x + 1, pl.ds(y, 1), :]

    def row_s(x):
        return lambda y: S[x + 1, pl.ds(y, 1), :]

    load_r.wait()

    def spike_loop(x, c):
        spike(x)
        return c

    lax.fori_loop(1, cx + 1, spike_loop, 0)
    load_s.wait()
    pack(lambda x: [row_r(f, x) for f in range(F)] + [row_s(x)], F + 1, 0)

    @pl.when(y_hi)
    def _():
        y_up.start()

    @pl.when(y_lo)
    def _():
        y_dn.start()

    @pl.when(y_lo)
    def _():
        y_up.wait_recv()

    @pl.when(y_hi)
    def _():
        y_dn.wait_recv()

    def unpack_first(x, c):
        for slot, y in ((0, TILE - 1), (1, TILE + cy)):
            for f in range(F):
                R[f, x + 1, pl.ds(y, 1), :] = got[slot, f, pl.ds(x, 1), :]
            S[x + 1, pl.ds(y, 1), :] = got[slot, F, pl.ds(x, 1), :]
        return c

    lax.fori_loop(0, cx, unpack_first, 0)

    lane = lax.broadcasted_iota(jnp.int32, (TILE, cz), 1)

    def add_grams(base, lefts, rights):
        for k, (i, j) in enumerate(PAIRS):
            prod = lefts[i] * rights[j]
            total = prod[:, :LANES]
            for c in range(LANES, cz, LANES):
                total = total + prod[:, c:c + LANES]
            acc[base + k] = acc[base + k] + total

    def apply(src, f, x, y, weights):
        mid = src[f, x, pl.ds(y, TILE), :]
        diag, xm, xp, ym, yp, zm, zp = weights
        out = diag * mid
        out = out - xm * src[f, x - 1, pl.ds(y, TILE), :]
        out = out - xp * src[f, x + 1, pl.ds(y, TILE), :]
        out = out - ym * src[f, x, pl.ds(y - 1, TILE), :]
        out = out - yp * src[f, x, pl.ds(y + 1, TILE), :]
        out = out - zm * pltpu.roll(mid, 1, axis=1)
        out = out - zp * pltpu.roll(mid, cz - 1, axis=1)
        return mid, out

    def tile_weights(x, t):
        y = TILE + t * TILE
        here = S[x, pl.ds(y, TILE), :]
        others = (
            S[x - 1, pl.ds(y, TILE), :],
            S[x + 1, pl.ds(y, TILE), :],
            S[x, pl.ds(y - 1, TILE), :],
            S[x, pl.ds(y + 1, TILE), :],
            jnp.where(lane == 0, 0.0, pltpu.roll(here, 1, axis=1)),
            jnp.where(lane == cz - 1, 0.0, pltpu.roll(here, cz - 1, axis=1)),
        )
        diag = jnp.zeros_like(here)
        weights = []
        for other in others:
            inside = other > 0.0
            mean = 0.5 * (here + other)
            diag = diag + jnp.where(inside, mean, here)
            weights.append(jnp.where(inside, mean, 0.0))
        weights = [diag] + weights
        for k in range(7):
            wt[k, x - 1, pl.ds(t * TILE, TILE), :] = weights[k]
        return weights

    def first_plane(x):
        for t in range(cy // TILE):
            y = TILE + t * TILE
            weights = tile_weights(x, t)
            rs, qs = [], []
            for f in range(F):
                mid, out = apply(R, f, x, y, weights)
                Q[f, x, pl.ds(y, TILE), :] = out
                rs.append(mid)
                qs.append(out)
            add_grams(0, rs, rs)
            add_grams(NP, rs, qs)

    def edge_weights(x):
        for t in range(cy // TILE):
            tile_weights(x, t)

    def edge_field(x, f):
        for t in range(cy // TILE):
            y = TILE + t * TILE
            weights = [wt[k, x - 1, pl.ds(t * TILE, TILE), :] for k in range(7)]
            Q[f, x, pl.ds(y, TILE), :] = apply(R, f, x, y, weights)[1]

    def edge_grams(x):
        for t in range(cy // TILE):
            y = TILE + t * TILE
            rs = [R[f, x, pl.ds(y, TILE), :] for f in range(F)]
            qs = [Q[f, x, pl.ds(y, TILE), :] for f in range(F)]
            add_grams(0, rs, rs)
            add_grams(NP, rs, qs)

    def second_plane(x):
        for t in range(cy // TILE):
            y = TILE + t * TILE
            weights = [wt[k, x - 1, pl.ds(t * TILE, TILE), :] for k in range(7)]
            qs, ws = [], []
            for f in range(F):
                mid, out = apply(Q, f, x, y, weights)
                W[f, x - 1, pl.ds(t * TILE, TILE), :] = out
                qs.append(mid)
                ws.append(out)
            add_grams(2 * NP, qs, qs)
            add_grams(3 * NP, qs, ws)

    def run(plane):
        def one(x, c):
            plane(x)
            return c
        return one

    lax.fori_loop(2, cx, run(first_plane), 0)

    def ends(plane):
        def one(k, c):
            plane(k)
            return c
        return one

    @pl.when(has_lo)
    def _():
        up_s.wait_recv()

    @pl.when(has_hi)
    def _():
        dn_s.wait_recv()

    lax.fori_loop(0, 2, ends(lambda k: edge_weights(1 + k * (cx - 1))), 0)

    for f in range(F):
        @pl.when(has_lo)
        def _():
            up_r[f].wait_recv()

        @pl.when(has_hi)
        def _():
            dn_r[f].wait_recv()

        lax.fori_loop(0, 2, ends(lambda k: spike(k * (cx + 1), (f,))), 0)
        lax.fori_loop(0, 2, ends(lambda k: edge_field(1 + k * (cx - 1), f)), 0)

        @pl.when(has_hi)
        def _():
            up_q[f].start()

        @pl.when(has_lo)
        def _():
            dn_q[f].start()

    pack(lambda x: [row_q(f, x) for f in range(F)], F, 2)

    @pl.when(y_hi)
    def _():
        y_up_q.start()

    @pl.when(y_lo)
    def _():
        y_dn_q.start()

    lax.fori_loop(0, 2, ends(lambda k: edge_grams(1 + k * (cx - 1))), 0)

    @pl.when(y_lo)
    def _():
        y_up_q.wait_recv()

    @pl.when(y_hi)
    def _():
        y_dn_q.wait_recv()

    def unpack_second(x, c):
        for slot, y in ((2, TILE - 1), (3, TILE + cy)):
            for f in range(F):
                Q[f, x + 1, pl.ds(y, 1), :] = got[slot, f, pl.ds(x, 1), :]
        return c

    lax.fori_loop(0, cx, unpack_second, 0)
    lax.fori_loop(2, cx, run(second_plane), 0)

    @pl.when(has_lo)
    def _():
        for copy in up_q:
            copy.wait_recv()

    @pl.when(has_hi)
    def _():
        for copy in dn_q:
            copy.wait_recv()

    lax.fori_loop(0, 2, ends(lambda k: second_plane(1 + k * (cx - 1))), 0)

    part_x[mx] = jnp.sum(acc[...], axis=1)

    def exchange(buf, axis, me, n, sends, recvs):
        copies = [
            remote(buf.at[me], buf.at[me], sends.at[d - 1], recvs.at[d - 1], axis, lax.rem(me + d, n))
            for d in range(1, n)
        ]
        for copy in copies:
            copy.start()
        for d in range(1, n):
            src = lax.rem(me + n - d, n)
            remote(
                buf.at[me], buf.at[src], sends.at[d - 1], recvs.at[d - 1], axis, src
            ).wait_recv()
        total = buf[0]
        for k in range(1, n):
            total = total + buf[k]
        return copies, total

    copies_x, total_x = exchange(part_x, "gx", mx, nx, ax_s, ax_r)
    part_y[my] = total_x
    copies_y, total = exchange(part_y, "gy", my, ny, ay_s, ay_r)
    sums[...] = jnp.broadcast_to(jnp.sum(total, axis=1, keepdims=True), sums.shape)

    for copy in copies_x + copies_y:
        copy.wait_send()

    @pl.when(has_hi)
    def _():
        up_s.wait_send()
        for copy in up_r + up_q:
            copy.wait_send()

    @pl.when(has_lo)
    def _():
        dn_s.wait_send()
        for copy in dn_r + dn_q:
            copy.wait_send()

    @pl.when(y_hi)
    def _():
        y_up.wait_send()
        y_up_q.wait_send()

    @pl.when(y_lo)
    def _():
        y_dn.wait_send()
        y_dn_q.wait_send()


def mat(a, b):
    return [
        [sum(a[i][k] * b[k][j] for k in range(1, F)) + a[i][0] * b[0][j] for j in range(F)]
        for i in range(F)
    ]


def add(a, b):
    return [[a[i][j] + b[i][j] for j in range(F)] for i in range(F)]


def sub(a, b):
    return [[a[i][j] - b[i][j] for j in range(F)] for i in range(F)]


def turn(a):
    return [[a[j][i] for j in range(F)] for i in range(F)]


def spd_solve(a, b):
    low = [[None] * F for _ in range(F)]
    inv = [None] * F
    rest = [list(row) for row in a]
    for k in range(F):
        inv[k] = 1.0 / rest[k][k]
        for i in range(k + 1, F):
            low[i][k] = rest[i][k] * inv[k]
        for i in range(k + 1, F):
            for j in range(k + 1, i + 1):
                rest[i][j] = rest[i][j] - low[i][k] * rest[j][k]
    out = [list(row) for row in b]
    for i in range(F):
        for k in range(i):
            out[i] = [u - low[i][k] * v for u, v in zip(out[i], out[k])]
    out = [[u * inv[i] for u in out[i]] for i in range(F)]
    for i in reversed(range(F)):
        for k in range(i + 1, F):
            out[i] = [u - low[k][i] * v for u, v in zip(out[i], out[k])]
    return out


def finish_kernel(sums, r_ref, q_ref, w_ref, x_ref, e_ref, coef):
    @pl.when(pl.program_id(0) == 0)
    def _():
        grams = []
        for g in range(4):
            m = [[None] * F for _ in range(F)]
            for k, (i, j) in enumerate(PAIRS):
                m[i][j] = m[j][i] = sums[pl.ds(g * NP + k, 1), :]
            grams.append(m)
        s0, s1, s2, s3 = grams
        a0 = spd_solve(s1, s0)
        s1a, s2a = mat(s1, a0), mat(s2, a0)
        a0t = turn(a0)
        rr = add(sub(sub(s0, s1a), turn(s1a)), mat(a0t, s2a))
        cross = add(sub(sub(s1, s2a), turn(s2a)), mat(a0t, mat(s3, a0)))
        beta = spd_solve(s0, rr)
        curve = sub(cross, mat(turn(beta), mat(s1, beta)))
        a1 = spd_solve(curve, rr)
        m1 = add(add(a0, a1), mat(beta, a1))
        m2 = mat(a0, a1)
        for i in range(F):
            for j in range(F):
                coef[pl.ds(i * F + j, 1), :] = m1[i][j]
                coef[pl.ds(F * F + i * F + j, 1), :] = m2[i][j]

    x = pl.program_id(0)
    cy, cz = w_ref.shape[2:]
    c1 = [[jnp.broadcast_to(coef[pl.ds(i * F + j, 1), :], (TILE, LANES)) for j in range(F)] for i in range(F)]
    c2 = [[jnp.broadcast_to(coef[pl.ds(F * F + i * F + j, 1), :], (TILE, LANES)) for j in range(F)] for i in range(F)]

    def tile(t, c):
        y = pl.ds(pl.multiple_of(t * TILE, TILE), TILE)
        wide_y = pl.ds(pl.multiple_of(t * TILE + TILE, TILE), TILE)
        for z in range(0, cz, LANES):
            at = pl.ds(z, LANES)
            rs = [r_ref[f, x + 1, wide_y, at] for f in range(F)]
            qs = [q_ref[f, x + 1, wide_y, at] for f in range(F)]
            ws = [w_ref[f, x, y, at] for f in range(F)]
            for j in range(F):
                field = rs[0] * c1[0][j] - qs[0] * c2[0][j]
                left = rs[j] - qs[0] * c1[0][j] + ws[0] * c2[0][j]
                for i in range(1, F):
                    field = field + rs[i] * c1[i][j] - qs[i] * c2[i][j]
                    left = left - qs[i] * c1[i][j] + ws[i] * c2[i][j]
                x_ref[j, 0, y, at] = field
                e_ref[j, 0, y, at] = left
        return c

    lax.fori_loop(0, cy // TILE, tile, 0)


def shards(nx, ny, adj, sig, elec):
    cx, cy, cz = sig.shape
    current = math.sqrt(nx * cx * ny * cy * cz)
    block = jax.ShapeDtypeStruct(adj.shape, jnp.float32)
    hbm = pl.BlockSpec(memory_space=pltpu.HBM)
    vmem = pl.BlockSpec(memory_space=pltpu.VMEM)
    padded = (cx + 2, cy + 2 * TILE, cz)
    wide = jax.ShapeDtypeStruct((F,) + padded, jnp.float32)
    dma = pltpu.SemaphoreType.DMA
    adj = pltpu.with_memory_space_constraint(adj, pltpu.HBM)
    sig = pltpu.with_memory_space_constraint(sig, pltpu.HBM)
    r, q, w, sums = pl.pallas_call(
        functools.partial(operator_kernel, nx, ny, current),
        out_shape=(wide, wide, block, jax.ShapeDtypeStruct((4 * NP, LANES), jnp.float32)),
        in_specs=[hbm, hbm, pl.BlockSpec(memory_space=pltpu.SMEM)],
        out_specs=(vmem, vmem, vmem, vmem),
        scratch_shapes=[
            pltpu.VMEM(padded, jnp.float32),
            pltpu.VMEM((7, cx, cy, cz), jnp.float32),
            pltpu.VMEM((4, F + 1, cx, cz), jnp.float32),
            pltpu.VMEM((4, F + 1, cx, cz), jnp.float32),
            pltpu.VMEM((4 * NP, TILE, LANES), jnp.float32),
            pltpu.VMEM((nx, 4 * NP, LANES), jnp.float32),
            pltpu.VMEM((ny, 4 * NP, LANES), jnp.float32),
            dma((2,)), dma((2 + 4 * F,)), dma((2 + 4 * F,)), dma((4,)), dma((4,)),
            dma((max(nx - 1, 1),)), dma((max(nx - 1, 1),)),
            dma((max(ny - 1, 1),)), dma((max(ny - 1, 1),)),
        ],
        compiler_params=pltpu.CompilerParams(collective_id=0, has_side_effects=True, vmem_limit_bytes=GRANT_A),
    )(adj, sig, elec)
    slab = pl.BlockSpec((F, 1, cy, cz), lambda x: (0, x, 0, 0))
    return pl.pallas_call(
        finish_kernel,
        grid=(cx,),
        out_shape=(block, block),
        in_specs=[vmem, vmem, vmem, vmem],
        out_specs=(slab, slab),
        scratch_shapes=[pltpu.VMEM((2 * F * F, LANES), jnp.float32)],
        compiler_params=pltpu.CompilerParams(vmem_limit_bytes=GRANT_B),
    )(sums, r, q, w)


def solution(mesh):
    placed = (P(None, "gx", "gy", None), P("gx", "gy", None), P())
    return jax.shard_map(
        functools.partial(shards, mesh.shape["gx"], mesh.shape["gy"]),
        mesh=mesh,
        in_specs=placed,
        out_specs=(P(None, "gx", "gy", None), P(None, "gx", "gy", None)),
        check_vma=False,
    )
```
